256 devices in a mesh: tm: 8 (over y, x_hi), dp: 32 (over x_lo, z, core).
Axes of the slice: x: 4 (x_hi: 2, x_lo: 2; x = x_hi * 2 + x_lo), y: 4, z: 8, core: 2. Of those that a mesh axis runs over, the one named last changes fastest.
Arguments:
- history: bfloat16 [32, 16384, 256], P('dp', 'tm'), may hold values from -6 to 6
- now_weight: bfloat16 [256, 1024], replicated, may hold values from -0.25 to 0.25
- past_weight: bfloat16 [256, 1024], replicated, may hold values from -0.25 to 0.25
- gate_bias: float32 [1024], replicated, may hold values from -1 to 1
- residual_weight: bfloat16 [512, 256], replicated, may hold values from -0.25 to 0.25
- skip_weight: bfloat16 [512, 256], replicated, may hold values from -0.25 to 0.25
- out_cotangent: bfloat16 [32, 16384, 256], P('dp', 'tm'), may hold values from -6 to 6
- skip_cotangent: bfloat16 [32, 16384, 256], P('dp', 'tm'), may hold values from -6 to 6
Outputs:
- residual_out: bfloat16 [32, 16384, 256], P('dp', 'tm')
- skip_out: bfloat16 [32, 16384, 256], P('dp', 'tm')
- grad_input: bfloat16 [32, 16384, 256], P('dp', 'tm')
- grad_now: float32 [256, 1024], P('dp')
- grad_past: float32 [256, 1024], P('dp')
- grad_bias: float32 [1024], P('dp')
- grad_residual: float32 [512, 256], P('dp')
- skip_grad: float32 [512, 256], P('dp')
The draws below stay inside these ranges and needn't reach their ends.
All inputs are finite; a program needn't handle non-finite values.
Results may differ from the reference program's by a relative error of at most 0.0048.
Values may be sent and summed in bfloat16 or wider, within the bound.
No kernel may reach another device: no remote copies, remote signals or barrier semaphores. Data moves between devices by JAX's collectives and lax.ppermute only.
A program may use at most 64 MiB of HBM per device.

```python
import jax
import jax.numpy as jnp
from jax import lax

RESIDUAL_WIDTH = 256
G = 512
DILATION_STEPS = 2048
B = 32
HISTORY_STEPS = 16384


def strengthened(values, own_key, source, target, blocks, factor):
    owner, partner = [(jnp.arange(values.shape[axis_at]) // (values.shape[axis_at] // blocks)).reshape([-1 if axis == axis_at else 1 for axis in range(values.ndim)]) for axis_at in (source, target)]
    chosen = jax.random.permutation(own_key, blocks)[partner]
    strong = (owner == chosen) | (owner == (partner + blocks // 2) % blocks)
    return jnp.where(strong, factor * values, values)


def block_scale(key, shape, split, smallest, top_value):
    def one(position, parts):
        draws = jax.random.uniform(jax.random.fold_in(jax.random.fold_in(key, 6), position), (parts,), jnp.float32, smallest / len(split), top_value / len(split))
        return jnp.repeat(jnp.exp(draws), shape[position] // parts).reshape((-1,) + (1,) * (len(shape) - position - 1))

    factor_of = one(*split[0])
    for cut in split[1:]:
        factor_of = factor_of * one(*cut)
    return factor_of


def gaussian(stream_key, shape, scale, limit, shards=(), kind=jnp.bfloat16):
    values = jax.random.normal(stream_key, shape, jnp.float32) * scale
    if len(shards) > 0:
        values = block_scale(stream_key, shape, shards, -0.22, 0.18) * values
    return jnp.clip(values, min=-limit, max=limit).astype(kind)


def noise_with(rng, dims, deviation, bound, pieces, heavy, kind=jnp.bfloat16):
    entries = deviation * jax.random.normal(rng, dims, jnp.float32)
    if pieces:
        entries = entries * block_scale(rng, dims, pieces, -0.22, 0.18)
    return jnp.clip(strengthened(entries, jax.random.fold_in(rng, 3), *heavy), -bound, bound).astype(kind)


def setup_inputs(seed: int = 0) -> dict:
    seeds = jax.random.split(jax.random.key(seed), 9)
    history = noise_with(seeds[0], (B, HISTORY_STEPS, RESIDUAL_WIDTH), 1.0, 6.0, ((0, 32), (1, 8)), (0, 2, 32, 2.75))
    now_weight = gaussian(seeds[1], (RESIDUAL_WIDTH, 2 * G), (2 * RESIDUAL_WIDTH) ** -0.5, 0.25)
    past_weight = gaussian(seeds[2], (RESIDUAL_WIDTH, 2 * G), (2 * RESIDUAL_WIDTH) ** -0.5, 0.25)
    gate_bias = jnp.clip(jax.random.uniform(seeds[3], (2 * G,), jnp.float32, -1.0, 1.0), -1.0, 1.0)
    residual_weight = gaussian(seeds[4], (G, RESIDUAL_WIDTH), G ** -0.5, 0.25)
    skip_weight = gaussian(seeds[5], (G, RESIDUAL_WIDTH), G ** -0.5, 0.25)
    out_cotangent = gaussian(seeds[6], (B, HISTORY_STEPS, RESIDUAL_WIDTH), 1.0, 6.0, ((0, 32), (1, 8)))
    skip_cotangent = gaussian(seeds[7], (B, HISTORY_STEPS, RESIDUAL_WIDTH), 1.0, 6.0, ((0, 32), (1, 8)))
    return dict(history=history, now_weight=now_weight, past_weight=past_weight, gate_bias=gate_bias, residual_weight=residual_weight, skip_weight=skip_weight, out_cotangent=out_cotangent, skip_cotangent=skip_cotangent)


def contract_rows(left, right):
    return lax.dot_general(left, right, (((0,), (0,)), ((), ())), preferred_element_type=jnp.float32)


def reference(history, now_weight, past_weight, gate_bias, residual_weight, skip_weight, out_cotangent, skip_cotangent):
    def one_history(carry, item):
        power_series, out_cot, skip_cot = item
        padding_rows = jnp.zeros((DILATION_STEPS, RESIDUAL_WIDTH), power_series.dtype)
        lagged_input = jnp.concatenate([padding_rows, power_series[:HISTORY_STEPS - DILATION_STEPS]], axis=0)
        zeta = jnp.dot(power_series, now_weight, preferred_element_type=jnp.float32)
        zeta = zeta + jnp.dot(lagged_input, past_weight, preferred_element_type=jnp.float32) + gate_bias
        tanh_part = jnp.tanh(zeta[:, :G])
        sigm_part = jax.nn.sigmoid(zeta[:, G:])
        gated = (tanh_part * sigm_part).astype(jnp.bfloat16)
        resid = (power_series.astype(jnp.float32) + jnp.dot(gated, residual_weight, preferred_element_type=jnp.float32)).astype(jnp.bfloat16)
        skipped = jnp.dot(gated, skip_weight, preferred_element_type=jnp.float32).astype(jnp.bfloat16)
        dgated = jnp.dot(out_cot, residual_weight.T, preferred_element_type=jnp.float32)
        dgated = dgated + jnp.dot(skip_cot, skip_weight.T, preferred_element_type=jnp.float32)
        dzeta = jnp.concatenate([dgated * sigm_part * (1.0 - tanh_part * tanh_part),
                                 dgated * tanh_part * sigm_part * (1.0 - sigm_part)], axis=1).astype(jnp.bfloat16)
        reverse_pass = jnp.dot(dzeta, past_weight.T, preferred_element_type=jnp.float32).astype(jnp.bfloat16)
        shifted_rows = jnp.concatenate([reverse_pass[DILATION_STEPS:], jnp.zeros((DILATION_STEPS, RESIDUAL_WIDTH), jnp.bfloat16)], axis=0)
        shifted_rows = lax.optimization_barrier(shifted_rows).astype(jnp.float32)
        grad_in = out_cot.astype(jnp.float32) + jnp.dot(dzeta, now_weight.T, preferred_element_type=jnp.float32) + shifted_rows
        grad_in = grad_in.astype(jnp.bfloat16)
        g_now, g_past, g_bias, g_res, g_skip = carry
        g_now = g_now + contract_rows(power_series, dzeta)
        g_past = g_past + contract_rows(lagged_input, dzeta)
        g_bias = g_bias + jnp.sum(dzeta.astype(jnp.float32), axis=0)
        g_res = g_res + contract_rows(gated, out_cot)
        g_skip = g_skip + contract_rows(gated, skip_cot)
        return (g_now, g_past, g_bias, g_res, g_skip), (resid, skipped, grad_in)

    start = (jnp.zeros((RESIDUAL_WIDTH, 2 * G), jnp.float32), jnp.zeros((RESIDUAL_WIDTH, 2 * G), jnp.float32),
             jnp.zeros((2 * G,), jnp.float32), jnp.zeros((G, RESIDUAL_WIDTH), jnp.float32), jnp.zeros((G, RESIDUAL_WIDTH), jnp.float32))
    sums, outputs = lax.scan(one_history, start, (history, out_cotangent, skip_cotangent))
    return (outputs[0], outputs[1], outputs[2], sums[0], sums[1], sums[2], sums[3], sums[4])
```

```python
import functools

import jax
import jax.numpy as jnp
from jax import lax
from jax.experimental import pallas as pl
from jax.experimental.pallas import tpu as pltpu
from jax.sharding import PartitionSpec as P

BF16, F32 = jnp.bfloat16, jnp.float32
TILE = 512
CHUNKS = (1024, 1024)
LANES = 128
CHIP_GROUPS = [[chip * 2 + core for chip in range(16)] for core in range(2)]


def dot(a, b):
    return jnp.dot(a, b, preferred_element_type=F32)


def rows_dot(a, b):
    return lax.dot_general(a, b, (((0,), (0,)), ((), ())), preferred_element_type=F32)


def layer_kernel(first, last, core, h, d, oc, sk, taps, bias, heads, heads_t, taps_t, *rest):
    n_in = 2 if first else 5
    outs = rest if first else rest[n_in:]
    if first:
        res, skip, part, back, g_taps, g_heads, g_bias = rest
    elif last:
        in_taps, in_heads, in_bias, _, _ = rest[:5]
        res, skip, part, back, send, keep, g_taps, g_heads, g_bias = rest[5:]
    width = h.shape[1]
    gated_width = 2 * width
    step = pl.program_id(0)

    @pl.when(step == 0)
    def _():
        if first:
            g_taps[...] = jnp.zeros_like(g_taps)
            g_heads[...] = jnp.zeros_like(g_heads)
            g_bias[...] = jnp.zeros_like(g_bias)
        else:
            g_taps[...] = in_taps[...]
            g_heads[...] = in_heads[...]
            g_bias[...] = in_bias[...]

    both = jnp.concatenate([h[...], d[...]], axis=1)
    cots = jnp.concatenate([oc[...], sk[...]], axis=1)
    z = dot(both, taps[...]) + bias[...]
    th = jnp.tanh(z[:, :gated_width])
    sg = 0.5 * jnp.tanh(0.5 * z[:, gated_width:]) + 0.5
    ts = th * sg
    gated = ts.astype(BF16)
    heads_out = dot(gated, heads[...])
    res[...] = (h[...].astype(F32) + heads_out[:, :width]).astype(BF16)
    skip[...] = heads_out[:, width:].astype(BF16)
    dg = dot(cots, heads_t[...])
    dza = dg * (sg - ts * th)
    dzb = dg * (ts - ts * sg)
    dz = jnp.concatenate([dza.astype(BF16), dzb.astype(BF16)], axis=1)
    down = dot(dz, taps_t[...])
    part[...] = oc[...].astype(F32) + down[:, :width]
    back[...] = down[:, width:].astype(BF16)
    g_taps[...] += rows_dot(both, dz)
    g_heads[...] += rows_dot(gated, cots)
    g_bias[...] += jnp.sum(dz.astype(F32).reshape(-1, 8, 2 * gated_width), axis=0)

    if last:

        @pl.when(step == pl.num_programs(0) - 1)
        def _():
            mine = core[0]
            for out, side in ((send, 1 - mine), (keep, mine)):
                for j in range(16):
                    r = pl.multiple_of((2 * j + side) * 8, 8)
                    rr = pl.multiple_of((2 * j + side) * 16, 16)
                    pieces = (
                        g_taps[pl.ds(r, 8), :],
                        g_taps[pl.ds(width + r, 8), :],
                        g_heads[pl.ds(rr, 8), :width],
                        g_heads[pl.ds(rr + 8, 8), :width],
                        g_heads[pl.ds(rr, 8), width:],
                        g_heads[pl.ds(rr + 8, 8), width:],
                        g_bias[:, (j // 2) * LANES : (j // 2 + 1) * LANES],
                    )
                    at = 0
                    for piece in pieces:
                        out[j, :, at : at + piece.shape[1]] = piece.astype(out.dtype)
                        at += piece.shape[1]


def layer(core, h, d, oc, sk, weights, base, rows, total, carry):
    first, last = base == 0, base + rows == total
    width = h.shape[1]
    tile = min(TILE, rows)
    off = base // tile
    taps, bias, heads, heads_t, taps_t = weights
    whole = pl.BlockSpec((tile, width), lambda i: (off + i, 0))
    own = pl.BlockSpec((tile, width), lambda i: (i, 0))
    const = lambda a: pl.BlockSpec(a.shape, lambda i: (0,) * len(a.shape))
    shape = lambda s, t: jax.ShapeDtypeStruct(s, t)
    ins = [core, h, d, oc, sk, taps, bias, heads, heads_t, taps_t]
    in_specs = [pl.BlockSpec(memory_space=pltpu.SMEM), whole, own, whole, whole]
    in_specs += [const(a) for a in ins[5:]]
    out_shape = [
        shape((total, width), BF16),
        shape((total, width), BF16),
        shape((rows, width), F32),
        shape((rows, width), BF16),
    ]
    out_specs = [whole, whole, own, own]
    sums = [shape((2 * width, 4 * width), F32), shape((2 * width, 2 * width), F32), shape((8, 4 * width), F32)]
    scratch, aliases = [], {}
    if first:
        out_shape += sums
        out_specs += [const(s) for s in sums]
    else:
        ins += list(carry)
        in_specs += [const(s) for s in sums] + [pl.BlockSpec(memory_space=pl.ANY)] * 2
        aliases = {13: 0, 14: 1}
        packed = (16, 8, 12 * width + LANES)
        out_shape += [shape(packed, BF16), shape(packed, F32)]
        out_specs += [const(s) for s in out_shape[4:]]
        scratch = [pltpu.VMEM(s.shape, F32) for s in sums]
    flops = 2 * rows * width * width * 36
    return pl.pallas_call(
        functools.partial(layer_kernel, first, last),
        out_shape=out_shape,
        grid=(rows // tile,),
        in_specs=in_specs,
        out_specs=out_specs,
        scratch_shapes=scratch,
        input_output_aliases=aliases,
        compiler_params=pltpu.CompilerParams(
            dimension_semantics=("arbitrary",), vmem_limit_bytes=50 << 20
        ),
        cost_estimate=pl.CostEstimate(
            flops=flops, bytes_accessed=rows * width * 20 + (6 << 20), transcendentals=4 * rows * width
        ),
        name="layer_rows",
    )(*ins)


def shift(value, steps):
    n = lax.axis_size("tm")
    return lax.ppermute(
        value, "tm", [(s, s + steps) for s in range(max(0, -steps), min(n, n - steps))]
    )


def shards(history, now_w, past_w, gate_bias, res_w, skip_w, out_cot, skip_cot):
    _, total, width = history.shape
    h, oc, sk = history[0], out_cot[0], skip_cot[0]
    dp = lax.axis_index("dp")
    core = jnp.reshape(dp % 2, (1,)).astype(jnp.int32)
    taps = jnp.concatenate([now_w, past_w], axis=0)
    heads = jnp.concatenate([res_w, skip_w], axis=1)
    weights = (taps, gate_bias[None, :], heads, heads.T, taps.T)

    bases = [sum(CHUNKS[:k]) for k in range(len(CHUNKS))]
    delayed = [shift(h[b : b + r], 1) for b, r in zip(bases, CHUNKS)]
    carry, parts, backs = None, [], []
    for b, r, d in zip(bases, CHUNKS, delayed):
        out = layer(core, h, d, oc, sk, weights, b, r, total, carry)
        res, skip, part, back = out[:4]
        parts.append(part)
        backs.append(shift(back, -1))
        carry = (*out[4:], res, skip)
    send, keep = out[4:]

    came = lax.ppermute(send, "dp", [(i, i ^ 1) for i in range(32)])
    pair = (keep + came.astype(F32)).astype(BF16)
    spread = lax.all_to_all(pair, "dp", 0, 0, axis_index_groups=CHIP_GROUPS)
    mine = jnp.sum(spread.astype(F32), axis=0)
    for k in (1, 2, 4):
        mine = mine + lax.ppermute(mine, "tm", [(i, i ^ k) for i in range(8)])

    grad_in = jnp.concatenate([p + b.astype(F32) for p, b in zip(parts, backs)], axis=0)
    g_now, g_past = mine[:, : 4 * width], mine[:, 4 * width : 8 * width]
    at = [8 * width + k * width for k in range(5)]
    tops = [mine[:, a : a + width] for a in at[:4]]
    g_res = jnp.concatenate(tops[:2], axis=0)
    g_skip = jnp.concatenate(tops[2:], axis=0)
    bias_sum = jnp.sum(mine[:, at[4] :], axis=0)
    g_bias = lax.dynamic_slice(bias_sum, ((dp % 4) * 32,), (32,))
    return (
        res[None],
        skip[None],
        grad_in.astype(BF16)[None],
        g_now,
        g_past,
        g_bias,
        g_res,
        g_skip,
    )


def solution(mesh):
    rows, whole = P("dp", "tm", None), P()
    return jax.shard_map(
        shards,
        mesh=mesh,
        in_specs=(rows, whole, whole, whole, whole, whole, rows, rows),
        out_specs=(rows, rows, rows, P("dp", None), P("dp", None), P("dp"), P("dp", None), P("dp", None)),
        check_vma=False,
    )
```

```python
import functools

import jax
import jax.numpy as jnp
from jax import lax
from jax.experimental import pallas as pl
from jax.experimental.pallas import tpu as pltpu
from jax.sharding import PartitionSpec as P

BF16, F32 = jnp.bfloat16, jnp.float32
TILE = 512
CHUNKS = (1024, 1024)
LANES = 128
VMEM = pl.BlockSpec(memory_space=pltpu.VMEM)


def dot(a, b):
    return jnp.dot(a, b, preferred_element_type=F32)


def dot_t(a, b):
    return lax.dot_general(a, b, (((1,), (1,)), ((), ())), preferred_element_type=F32)


def dot_rows(a, b):
    return lax.dot_general(a, b, (((0,), (0,)), ((), ())), preferred_element_type=F32)


def tile_rows(base=0):
    return pl.ds(pl.multiple_of(base + pl.program_id(0) * TILE, TILE), TILE)


def before_kernel(h, oc, sk, now_w, bias, res_w, skip_w, z_now, dg):
    rows = tile_rows()
    z_now[rows, :] = dot(h[rows, :], now_w[...]) + bias[...]
    dg[rows, :] = dot_t(oc[rows, :], res_w[...]) + dot_t(sk[rows, :], skip_w[...])


def gates(base, h, d, oc, sk, z_now, dg, past_w, g_taps, g_heads, g_bias):
    rows = tile_rows(base)
    delayed = d[tile_rows(), :]
    z = z_now[rows, :] + dot(delayed, past_w[...])
    half = z.shape[1] // 2
    th = jnp.tanh(z[:, :half])
    sg = 0.5 * jnp.tanh(0.5 * z[:, half:]) + 0.5
    ts = th * sg
    gated = ts.astype(BF16)
    dgated = dg[rows, :]
    dza = dgated * (sg - ts * th)
    dzb = dgated * (ts - ts * sg)
    dz = jnp.concatenate([dza.astype(BF16), dzb.astype(BF16)], axis=1)
    g_taps[...] += dot_rows(jnp.concatenate([h[rows, :], delayed], axis=1), dz)
    g_heads[...] += dot_rows(gated, jnp.concatenate([oc[rows, :], sk[rows, :]], axis=1))
    g_bias[...] += jnp.sum(dz.astype(F32).reshape(-1, 8, 2 * half), axis=0)
    return gated, dz


def results(base, gated, dz, h, oc, now_w, past_w, res_w, skip_w, res, skip, part, back):
    rows = tile_rows(base)
    res[...] = (h[rows, :].astype(F32) + dot(gated, res_w[...])).astype(BF16)
    skip[...] = dot(gated, skip_w[...]).astype(BF16)
    part[...] = oc[rows, :].astype(F32) + dot_t(dz, now_w[...])
    back[...] = dot_t(dz, past_w[...]).astype(BF16)


def first_kernel(h, d, oc, sk, z_now, dg, now_w, past_w, res_w, skip_w, *outs):
    res, skip, part, back, g_taps, g_heads, g_bias = outs

    @pl.when(pl.program_id(0) == 0)
    def _():
        for g in (g_taps, g_heads, g_bias):
            g[...] = jnp.zeros_like(g)

    gated, dz = gates(0, h, d, oc, sk, z_now, dg, past_w, g_taps, g_heads, g_bias)
    results(0, gated, dz, h, oc, now_w, past_w, res_w, skip_w, res, skip, part, back)


def last_kernel(base, place, h, d, oc, sk, z_now, dg, past_w, *rest):
    gated, dz, send, keep, g_taps, g_heads, g_bias = rest[3:]
    rows = tile_rows()
    gated[rows, :], dz[rows, :] = gates(
        base, h, d, oc, sk, z_now, dg, past_w, g_taps, g_heads, g_bias
    )
    width = h.shape[1]

    @pl.when(pl.program_id(0) == pl.num_programs(0) - 1)
    def _():
        mine = place[0]
        for out, side in ((send, 1 - mine), (keep, mine)):
            for chip in range(16):
                x_lo, z = divmod(chip, 8)
                r = pl.multiple_of((2 * chip + side) * 8, 8)
                rr = pl.multiple_of((2 * chip + side) * 16, 16)
                pieces = (
                    g_taps[pl.ds(r, 8), :],
                    g_taps[pl.ds(width + r, 8), :],
                    g_heads[pl.ds(rr, 8), :width],
                    g_heads[pl.ds(rr + 8, 8), :width],
                    g_heads[pl.ds(rr, 8), width:],
                    g_heads[pl.ds(rr + 8, 8), width:],
                    g_bias[:, (chip // 2) * LANES : (chip // 2 + 1) * LANES],
                )
                at = 0
                for piece in pieces:
                    out[z % 2, z // 2, x_lo, :, at : at + piece.shape[1]] = piece.astype(out.dtype)
                    at += piece.shape[1]


def by_core_kernel(place, keep, came, keep_next, send_next):
    for out, odd in ((keep_next, place[1]), (send_next, 1 - place[1])):
        out[...] = (keep[odd] + came[odd].astype(F32)).astype(out.dtype)


def by_pair_kernel(place, keep, came, *outs):
    for k, out in enumerate(outs):
        at = lax.rem(place[2] + k, 4)
        out[...] = (keep[at] + came[at].astype(F32)).astype(out.dtype)


def total_of(own, one, two, three):
    return (own.astype(F32) + two.astype(F32)) + (one.astype(F32) + three.astype(F32))


def by_z_kernel(place, own, one, two, three, same, other):
    for out, at in ((same, place[3]), (other, 1 - place[3])):
        out[...] = total_of(own[at], one[at], two[at], three[at])


def by_x_kernel(own, one, two, three, out):
    out[...] = total_of(own[...], one[...], two[...], three[...])


def owner_kernel(place, own, one, two, three, g_now, g_past, g_res, g_skip, g_bias):
    width = g_res.shape[1]
    total = lambda at, n: total_of(*(a[:, at : at + n] for a in (own, one, two, three)))
    g_now[...] = total(0, 4 * width)
    g_past[...] = total(4 * width, 4 * width)
    for k in range(2):
        g_res[8 * k : 8 * k + 8, :] = total((8 + k) * width, width)
        g_skip[8 * k : 8 * k + 8, :] = total((10 + k) * width, width)
    sums = jnp.sum(total(12 * width, LANES), axis=0, keepdims=True)
    for m in range(4):

        @pl.when(place[4] == m)
        def _():
            g_bias[...] = sums[:, m * 32 : (m + 1) * 32]


def after_kernel(base, gated, dz, h, oc, now_w, past_w, res_w, skip_w, *rest):
    rows = tile_rows()
    results(base, gated[rows, :], dz[rows, :], h, oc, now_w, past_w, res_w, skip_w, *rest[4:])


def finish_kernel(part, came, out):
    out[...] = (part[...] + came[...].astype(F32)).astype(BF16)


def call(body, name, steps, ins, in_specs, outs, out_specs, flops, aliases={}):
    return pl.pallas_call(
        body,
        out_shape=[kind(s, t) for s, t, *_ in outs for kind in [pltpu.HBM if _ else jax.ShapeDtypeStruct]],
        grid=(steps,),
        in_specs=in_specs,
        out_specs=out_specs,
        input_output_aliases=aliases,
        compiler_params=pltpu.CompilerParams(
            dimension_semantics=("arbitrary",), vmem_limit_bytes=24 << 20
        ),
        cost_estimate=pl.CostEstimate(flops=flops, bytes_accessed=flops >> 9, transcendentals=0),
        name=name,
    )(*ins)


def in_hbm(value):
    return pltpu.with_memory_space_constraint(value, pltpu.HBM)


def shift(value, steps):
    n = lax.axis_size("tm")
    return lax.ppermute(
        value, "tm", [(s, s + steps) for s in range(max(0, -steps), min(n, n - steps))]
    )


def exchange(value, axis, partner):
    return lax.ppermute(value, axis, [(i, partner(i)) for i in range(lax.axis_size(axis))])


def along_z(value, target):
    return exchange(value, "dp", lambda i: i // 16 * 16 + target(i // 2 % 8) * 2 + i % 2)


def along_y(value, k):
    return exchange(value, "tm", lambda i: (i + 2 * k) % 8)


def along_x(value, k):
    def target(i):
        x = (i // 32 % 2 * 2 + i % 32 // 16 + k) % 4
        return i // 64 * 64 + x // 2 * 32 + x % 2 * 16 + i % 16

    return lax.ppermute(value, ("tm", "dp"), [(i, target(i)) for i in range(256)])


def shards(history, now_w, past_w, gate_bias, res_w, skip_w, out_cot, skip_cot):
    _, total, width = history.shape
    h, oc, sk = history[0], out_cot[0], skip_cot[0]
    dp = lax.axis_index("dp")
    z = (dp // 2) % 8
    place = jnp.stack([dp % 2, z % 2, z // 2, dp // 16, dp % 4]).astype(jnp.int32)
    first, last = CHUNKS
    macs = 2 * total * width * width

    h_first = h[:first]
    h, h_first = lax.optimization_barrier((h, h_first))
    d_first = shift(h_first, 1)
    d_last = shift(h[first:], 1)

    z_now, dg = call(
        before_kernel,
        "before",
        total // TILE,
        (h, oc, sk, now_w, gate_bias[None, :], res_w, skip_w),
        [VMEM] * 7,
        [((total, 4 * width), F32), ((total, 2 * width), F32)],
        [VMEM] * 2,
        macs * 8,
    )
    sums = [((2 * width, 4 * width), F32), ((2 * width, 2 * width), F32), ((8, 4 * width), F32)]
    rows_out = [
        ((total, width), BF16),
        ((total, width), BF16),
        ((total, width), F32, 1),
        ((total, width), BF16, 1),
    ]
    block = lambda base: pl.BlockSpec((TILE, width), lambda i: (base // TILE + i, 0))
    *outs, g_taps, g_heads, g_bias = call(
        first_kernel,
        "first",
        first // TILE,
        (h, d_first, oc, sk, z_now, dg, now_w, past_w, res_w, skip_w),
        [VMEM] * 10,
        rows_out + sums,
        [block(0)] * 4 + [VMEM] * 3,
        macs * 28 * first // total,
    )
    block_shape = (8, 12 * width + LANES)
    packed = (2, 4, 2, *block_shape)
    gated, dz, send, keep, *_ = call(
        functools.partial(last_kernel, first),
        "last",
        last // TILE,
        (place, h, d_last, oc, sk, z_now, dg, past_w, g_taps, g_heads, g_bias),
        [pl.BlockSpec(memory_space=pltpu.SMEM)] + [VMEM] * 10,
        [((last, 2 * width), BF16), ((last, 4 * width), BF16), (packed, BF16), (packed, F32)] + sums,
        [VMEM] * 7,
        macs * 16 * last // total,
        {8: 4, 9: 5, 10: 6},
    )
    came = exchange(send, "dp", lambda i: i ^ 1)
    res, skip, part, back = call(
        functools.partial(after_kernel, first),
        "after",
        last // TILE,
        (gated, dz, h, oc, now_w, past_w, res_w, skip_w, *outs),
        [VMEM] * 8 + [pl.BlockSpec(memory_space=pl.ANY)] * 4,
        rows_out,
        [block(first)] * 4,
        macs * 12 * last // total,
        {8: 0, 9: 1, 10: 2, 11: 3},
    )
    came, back = lax.optimization_barrier((came, back))
    smem = pl.BlockSpec(memory_space=pltpu.SMEM)
    step = lambda body, name, ins, outs: call(
        body, name, 1, ins, [smem] * (ins[0] is place) + [VMEM] * (len(ins) - (ins[0] is place)), outs,
        [VMEM] * len(outs), 1 << 20,
    )
    keep, send = step(by_core_kernel, "by_core", (place, keep, came), [(packed[1:], F32), (packed[1:], BF16)])
    came = along_z(send, lambda z: z ^ 1)
    own, *others = step(
        by_pair_kernel, "by_pair", (place, keep, came), [(packed[2:], F32)] + [(packed[2:], BF16)] * 3
    )
    one, two, three = (along_z(v, lambda z, k=k: (z + 2 * k) % 8) for k, v in enumerate(others, 1))
    (grad_in,) = call(
        finish_kernel,
        "finish",
        total // TILE,
        (part, shift(back, -1)),
        [block(0)] * 2,
        [((total, width), BF16)],
        [block(0)],
        macs * 1000,
    )
    own, one, two, three, grad_in = lax.optimization_barrier((own, one, two, three, grad_in))
    same, other = step(
        by_z_kernel, "by_z", (place, own, one, two, three), [(block_shape, F32)] * 2
    )
    (mine,) = step(
        by_x_kernel, "by_x", (same, along_x(other, 1), along_x(same, 2), along_x(other, 3)), [(block_shape, F32)]
    )
    g_now, g_past, g_res, g_skip, g_bias = step(
        owner_kernel,
        "owner",
        (place, mine, *(along_y(mine, k) for k in (1, 2, 3))),
        [((8, 4 * width), F32)] * 2 + [((16, width), F32)] * 2 + [((1, 32), F32)],
    )
    return res[None], skip[None], grad_in[None], g_now, g_past, g_bias[0], g_res, g_skip


def solution(mesh):
    rows, whole = P("dp", "tm", None), P()
    return jax.shard_map(
        shards,
        mesh=mesh,
        in_specs=(rows, whole, whole, whole, whole, whole, rows, rows),
        out_specs=(rows, rows, rows, P("dp", None), P("dp", None), P("dp"), P("dp", None), P("dp", None)),
        check_vma=False,
    )
```

```python
import functools

import jax
import jax.numpy as jnp
from jax import lax
from jax.experimental import pallas as pl
from jax.experimental.pallas import tpu as pltpu
from jax.sharding import PartitionSpec as P

BF16, F32 = jnp.bfloat16, jnp.float32
TILE = 512
CHUNKS = (1024, 1024)
LANES = 128
VMEM = pl.BlockSpec(memory_space=pltpu.VMEM)


def dot(a, b):
    return jnp.dot(a, b, preferred_element_type=F32)


def dot_t(a, b):
    return lax.dot_general(a, b, (((1,), (1,)), ((), ())), preferred_element_type=F32)


def dot_rows(a, b):
    return lax.dot_general(a, b, (((0,), (0,)), ((), ())), preferred_element_type=F32)


def tile_rows(base=0):
    return pl.ds(pl.multiple_of(base + pl.program_id(0) * TILE, TILE), TILE)


def before_kernel(h, oc, sk, now_w, bias, res_w, skip_w, z_now, dg):
    rows = tile_rows()
    z_now[rows, :] = dot(h[...], now_w[...]) + bias[...]
    dg[rows, :] = dot_t(oc[...], res_w[...]) + dot_t(sk[...], skip_w[...])


def gates(base, h, d, oc, sk, z_now, dg, past_w, g_taps, g_heads, g_bias):
    rows = tile_rows(base)
    delayed = d[tile_rows(), :]
    z = z_now[rows, :] + dot(delayed, past_w[...])
    half = z.shape[1] // 2
    th = jnp.tanh(z[:, :half])
    sg = 0.5 * jnp.tanh(0.5 * z[:, half:]) + 0.5
    ts = th * sg
    gated = ts.astype(BF16)
    dgated = dg[rows, :]
    dza = dgated * (sg - ts * th)
    dzb = dgated * (ts - ts * sg)
    dz = jnp.concatenate([dza.astype(BF16), dzb.astype(BF16)], axis=1)
    g_taps[...] += dot_rows(jnp.concatenate([h[rows, :], delayed], axis=1), dz)
    g_heads[...] += dot_rows(gated, jnp.concatenate([oc[rows, :], sk[rows, :]], axis=1))
    g_bias[...] += jnp.sum(dz.astype(F32).reshape(-1, 8, 2 * half), axis=0)
    return gated, dz


def results(base, gated, dz, h, oc, now_w, past_w, res_w, skip_w, res, skip, part, back):
    rows = tile_rows(base)
    res[...] = (h[rows, :].astype(F32) + dot(gated, res_w[...])).astype(BF16)
    skip[...] = dot(gated, skip_w[...]).astype(BF16)
    part[...] = oc[rows, :].astype(F32) + dot_t(dz, now_w[...])
    back[...] = dot_t(dz, past_w[...]).astype(BF16)


def first_kernel(h, d, oc, sk, z_now, dg, now_w, past_w, res_w, skip_w, *outs):
    res, skip, part, back, g_taps, g_heads, g_bias = outs

    @pl.when(pl.program_id(0) == 0)
    def _():
        for g in (g_taps, g_heads, g_bias):
            g[...] = jnp.zeros_like(g)

    gated, dz = gates(0, h, d, oc, sk, z_now, dg, past_w, g_taps, g_heads, g_bias)
    results(0, gated, dz, h, oc, now_w, past_w, res_w, skip_w, res, skip, part, back)


def last_kernel(base, place, h, d, oc, sk, z_now, dg, past_w, *rest):
    gated, dz, send0, send1, keep, g_taps, g_heads, g_bias = rest[3:]
    rows = tile_rows()
    gated[rows, :], dz[rows, :] = gates(
        base, h, d, oc, sk, z_now, dg, past_w, g_taps, g_heads, g_bias
    )
    width = h.shape[1]

    @pl.when(pl.program_id(0) == pl.num_programs(0) - 1)
    def _():
        mine = place[0]
        for outs, side in (((send0, send1), 1 - mine), ((keep.at[0], keep.at[1]), mine)):
            for chip in range(16):
                x_lo, z = divmod(chip, 8)
                r = pl.multiple_of((2 * chip + side) * 8, 8)
                rr = pl.multiple_of((2 * chip + side) * 16, 16)
                pieces = (
                    g_taps[pl.ds(r, 8), :],
                    g_taps[pl.ds(width + r, 8), :],
                    g_heads[pl.ds(rr, 8), :width],
                    g_heads[pl.ds(rr + 8, 8), :width],
                    g_heads[pl.ds(rr, 8), width:],
                    g_heads[pl.ds(rr + 8, 8), width:],
                    g_bias[:, (chip // 2) * LANES : (chip // 2 + 1) * LANES],
                )
                at = 0
                for piece in pieces:
                    outs[z % 2][z // 2, x_lo, :, at : at + piece.shape[1]] = piece.astype(outs[0].dtype)
                    at += piece.shape[1]


def by_core_kernel(place, keep, came0, came1, keep_next, send_next):
    for odd, (near, far) in enumerate(((came0, came1), (came1, came0))):

        @pl.when(place[1] == odd)
        def _():
            keep_next[...] = keep[odd] + near[...].astype(F32)
            send_next[...] = (keep[1 - odd] + far[...].astype(F32)).astype(BF16)


def by_pair_kernel(place, keep, came, *outs):
    for k, out in enumerate(outs):
        at = lax.rem(place[2] + k, 4)
        out[...] = (keep[at] + came[at].astype(F32)).astype(out.dtype)


def total_of(own, one, two, three):
    return (own.astype(F32) + two.astype(F32)) + (one.astype(F32) + three.astype(F32))


def by_z_kernel(place, own, one, two, three, same, other):
    for out, at in ((same, place[3]), (other, 1 - place[3])):
        out[...] = total_of(own[at], one[at], two[at], three[at]).astype(out.dtype)


def by_x_kernel(own, one, two, three, out):
    out[...] = total_of(own[...], one[...], two[...], three[...]).astype(out.dtype)


def owner_kernel(place, own, one, two, three, g_now, g_past, g_res, g_skip, g_bias):
    width = g_res.shape[1]
    total = lambda at, n: total_of(*(a[:, at : at + n] for a in (own, one, two, three)))
    g_now[...] = total(0, 4 * width)
    g_past[...] = total(4 * width, 4 * width)
    for k in range(2):
        g_res[8 * k : 8 * k + 8, :] = total((8 + k) * width, width)
        g_skip[8 * k : 8 * k + 8, :] = total((10 + k) * width, width)
    sums = jnp.sum(total(12 * width, LANES), axis=0, keepdims=True)
    for m in range(4):

        @pl.when(place[4] == m)
        def _():
            g_bias[...] = sums[:, m * 32 : (m + 1) * 32]


def after_kernel(base, gated, dz, h, oc, now_w, past_w, res_w, skip_w, *rest):
    rows = tile_rows()
    results(base, gated[rows, :], dz[rows, :], h, oc, now_w, past_w, res_w, skip_w, *rest[2:])


def finish_kernel(part, came, *refs):
    refs[-1][...] = (part[...] + came[...].astype(F32)).astype(BF16)


def call(body, name, steps, ins, in_specs, outs, out_specs, flops, aliases={}):
    return pl.pallas_call(
        body,
        out_shape=[kind(s, t) for s, t, *_ in outs for kind in [pltpu.HBM if _ else jax.ShapeDtypeStruct]],
        grid=(steps,),
        in_specs=in_specs,
        out_specs=out_specs,
        input_output_aliases=aliases,
        compiler_params=pltpu.CompilerParams(
            dimension_semantics=("arbitrary",), vmem_limit_bytes=24 << 20
        ),
        cost_estimate=pl.CostEstimate(flops=flops, bytes_accessed=flops >> 9, transcendentals=0),
        name=name,
    )(*ins)


def in_hbm(value):
    return pltpu.with_memory_space_constraint(value, pltpu.HBM)


def copy_rows_kernel(base, src, dst, sem):
    copy = pltpu.make_async_copy(src.at[pl.ds(base, dst.shape[0]), :], dst, sem)
    copy.start()
    copy.wait()


def copy_rows(value, base, rows):
    return pl.pallas_call(
        functools.partial(copy_rows_kernel, base),
        out_shape=jax.ShapeDtypeStruct((rows, value.shape[1]), value.dtype),
        in_specs=[pl.BlockSpec(memory_space=pl.ANY)],
        out_specs=VMEM,
        scratch_shapes=[pltpu.SemaphoreType.DMA],
        cost_estimate=pl.CostEstimate(flops=0, bytes_accessed=1 << 20, transcendentals=0),
        name="copy_rows",
    )(in_hbm(value))


def shift(value, steps):
    n = lax.axis_size("tm")
    return lax.ppermute(
        value, "tm", [(s, s + steps) for s in range(max(0, -steps), min(n, n - steps))]
    )


def exchange(value, axis, partner):
    return lax.ppermute(value, axis, [(i, partner(i)) for i in range(lax.axis_size(axis))])


def along_z(value, target):
    return exchange(value, "dp", lambda i: i // 16 * 16 + target(i // 2 % 8) * 2 + i % 2)


def along_y(value, k):
    return exchange(value, "tm", lambda i: (i + 2 * k) % 8)


def along_x(value, k):
    def target(i):
        x = (i // 32 % 2 * 2 + i % 32 // 16 + k) % 4
        return i // 64 * 64 + x // 2 * 32 + x % 2 * 16 + i % 16

    return lax.ppermute(value, ("tm", "dp"), [(i, target(i)) for i in range(256)])


def shards(history, now_w, past_w, gate_bias, res_w, skip_w, out_cot, skip_cot):
    _, total, width = history.shape
    h, oc, sk = history[0], out_cot[0], skip_cot[0]
    dp = lax.axis_index("dp")
    z = (dp // 2) % 8
    place = jnp.stack([dp % 2, z % 2, z // 2, dp // 16, dp % 4]).astype(jnp.int32)
    place, gate_bias = lax.optimization_barrier((place, gate_bias))
    first, last = CHUNKS
    macs = 2 * total * width * width

    d_first = shift(copy_rows(h, 0, first), 1)
    d_last = shift(copy_rows(h, first, last), 1)

    z_now, dg = call(
        before_kernel,
        "before",
        total // TILE,
        tuple(in_hbm(a) for a in (h, oc, sk, now_w, gate_bias[None, :], res_w, skip_w)),
        [pl.BlockSpec((TILE, width), lambda i: (i, 0))] * 3
        + [pl.BlockSpec(s, lambda i: (0, 0)) for s in (now_w.shape, (1, 4 * width), res_w.shape, skip_w.shape)],
        [((total, 4 * width), F32), ((total, 2 * width), F32)],
        [VMEM] * 2,
        macs * 8,
    )
    sums = [((2 * width, 4 * width), F32), ((2 * width, 2 * width), F32), ((8, 4 * width), F32)]
    rows_out = [
        ((total, width), BF16),
        ((total, width), BF16),
    ]
    tail_out = lambda n: [((n, width), F32, 1), ((n, width), BF16)]
    block = lambda base: pl.BlockSpec((TILE, width), lambda i: (base // TILE + i, 0))
    res, skip, part0, back0, g_taps, g_heads, g_bias = call(
        first_kernel,
        "first",
        first // TILE,
        (h, d_first, oc, sk, z_now, dg, now_w, past_w, res_w, skip_w),
        [VMEM] * 10,
        rows_out + tail_out(first) + sums,
        [block(0)] * 4 + [VMEM] * 3,
        macs * 28 * first // total,
    )
    block_shape = (8, 12 * width + LANES)
    packed = (2, 4, 2, *block_shape)
    came0 = shift(back0, -1)
    gated, dz, send0, send1, keep, *_ = call(
        functools.partial(last_kernel, first),
        "last",
        last // TILE,
        (place, h, d_last, oc, sk, z_now, dg, past_w, g_taps, g_heads, g_bias),
        [pl.BlockSpec(memory_space=pltpu.SMEM)] + [VMEM] * 10,
        [((last, 2 * width), BF16), ((last, 4 * width), BF16), (packed[1:], BF16), (packed[1:], BF16), (packed, F32)]
        + sums,
        [VMEM] * 8,
        1 << 20,
        {8: 5, 9: 6, 10: 7},
    )
    halves = [exchange(v, "dp", lambda i: i ^ 1) for v in (send0, send1)]
    *halves, came0 = lax.optimization_barrier((*halves, came0))
    smem = pl.BlockSpec(memory_space=pltpu.SMEM)
    step = lambda body, name, ins, outs, flops=1 << 20: call(
        body, name, 1, ins, [smem] * (ins[0] is place) + [VMEM] * (len(ins) - (ins[0] is place)), outs,
        [VMEM] * len(outs), flops,
    )
    keep, send = step(by_core_kernel, "by_core", (place, keep, *halves), [(packed[1:], F32), (packed[1:], BF16)])
    came = along_z(send, lambda z: z ^ 1)
    gated, dz, _ = lax.optimization_barrier((gated, dz, send))
    res, skip, part1, back1 = call(
        functools.partial(after_kernel, first),
        "after",
        last // TILE,
        (gated, dz, h, oc, now_w, past_w, res_w, skip_w, res, skip),
        [VMEM] * 8 + [pl.BlockSpec(memory_space=pl.ANY)] * 2,
        rows_out + tail_out(last),
        [block(first)] * 2 + [block(0)] * 2,
        macs * 12 * last // total,
        {8: 0, 9: 1},
    )

    own, *others = step(
        by_pair_kernel, "by_pair", (place, keep, came), [(packed[2:], F32)] + [(packed[2:], BF16)] * 3,
        macs * 1000,
    )
    one, two, three = (along_z(v, lambda z, k=k: (z + 2 * k) % 8) for k, v in enumerate(others, 1))
    finish = lambda base, rows, ins, aliases: call(
        finish_kernel, "finish", rows // TILE, ins,
        [block(0)] * 2 + [pl.BlockSpec(memory_space=pl.ANY)] * len(aliases),
        [((total, width), BF16)], [block(base)], macs, aliases,
    )[0]
    grad_in = finish(0, first, (part0, came0), {})
    own, one, two, three, grad_in = lax.optimization_barrier((own, one, two, three, grad_in))
    grad_in = finish(first, last, (part1, shift(back1, -1), grad_in), {2: 0})
    same, other = step(
        by_z_kernel, "by_z", (place, own, one, two, three), [(block_shape, BF16)] * 2
    )
    (mine,) = step(
        by_x_kernel, "by_x", (same, along_x(other, 1), along_x(same, 2), along_x(other, 3)), [(block_shape, BF16)]
    )
    others = [along_y(mine, k) for k in (1, 2, 3)]
    *others, grad_in = lax.optimization_barrier((*others, grad_in))
    g_now, g_past, g_res, g_skip, g_bias = step(
        owner_kernel,
        "owner",
        (place, mine, *others),
        [((8, 4 * width), F32)] * 2 + [((16, width), F32)] * 2 + [((1, 32), F32)],
    )
    return res[None], skip[None], grad_in[None], g_now, g_past, g_bias[0], g_res, g_skip


def solution(mesh):
    rows, whole = P("dp", "tm", None), P()
    return jax.shard_map(
        shards,
        mesh=mesh,
        in_specs=(rows, whole, whole, whole, whole, whole, rows, rows),
        out_specs=(rows, rows, rows, P("dp", None), P("dp", None), P("dp"), P("dp", None), P("dp", None)),
        check_vma=False,
    )
```

```python
import functools

import jax
import jax.numpy as jnp
from jax import lax
from jax.experimental import pallas as pl
from jax.experimental.pallas import tpu as pltpu
from jax.sharding import PartitionSpec as P

BF16, F32 = jnp.bfloat16, jnp.float32
TILE = 512
CHUNKS = (1024, 1024)
LANES = 128
VMEM = pl.BlockSpec(memory_space=pltpu.VMEM)


def dot(a, b):
    return jnp.dot(a, b, preferred_element_type=F32)


def dot_t(a, b):
    return lax.dot_general(a, b, (((1,), (1,)), ((), ())), preferred_element_type=F32)


def dot_rows(a, b):
    return lax.dot_general(a, b, (((0,), (0,)), ((), ())), preferred_element_type=F32)


def tile_rows(base=0):
    return pl.ds(pl.multiple_of(base + pl.program_id(0) * TILE, TILE), TILE)


def before_kernel(h, oc, sk, now_w, bias, res_w, skip_w, z_now, dg):
    rows = tile_rows()
    z_now[rows, :] = dot(h[...], now_w[...]) + bias[...]
    dg[rows, :] = dot_t(oc[...], res_w[...]) + dot_t(sk[...], skip_w[...])


def gates(base, d, z_now, dg, past_w):
    rows = tile_rows(base)
    z = z_now[rows, :] + dot(d[tile_rows(), :], past_w[...])
    half = z.shape[1] // 2
    th = jnp.tanh(z[:, :half])
    sg = 0.5 * jnp.tanh(0.5 * z[:, half:]) + 0.5
    ts = th * sg
    dgated = dg[rows, :]
    dza = dgated * (sg - ts * th)
    dzb = dgated * (ts - ts * sg)
    return ts.astype(BF16), jnp.concatenate([dza.astype(BF16), dzb.astype(BF16)], axis=1)


def weight_sums(base, gated, dz, h, d, oc, sk, g_taps, g_heads, g_bias):
    rows = tile_rows(base)
    inputs = jnp.concatenate([h[rows, :], d[tile_rows(), :]], axis=1)
    g_taps[...] += dot_rows(inputs, dz)
    g_heads[...] += dot_rows(gated, jnp.concatenate([oc[rows, :], sk[rows, :]], axis=1))
    g_bias[...] += jnp.sum(dz.astype(F32).reshape(-1, 8, dz.shape[1]), axis=0)


def results(base, gated, dz, h, oc, now_w, res_w, skip_w, res, skip, part):
    rows = tile_rows(base)
    res[...] = (h[rows, :].astype(F32) + dot(gated, res_w[...])).astype(BF16)
    skip[...] = dot(gated, skip_w[...]).astype(BF16)
    part[...] = oc[rows, :].astype(F32) + dot_t(dz, now_w[...])


def first_kernel(d, z_now, dg, past_w, back, gated, dz):
    rows = tile_rows()
    gated_rows, dz_rows = gates(0, d, z_now, dg, past_w)
    back[...] = dot_t(dz_rows, past_w[...]).astype(BF16)
    gated[rows, :], dz[rows, :] = gated_rows, dz_rows


def rest_kernel(gated, dz, h, d, oc, sk, now_w, res_w, skip_w, *outs):
    res, skip, part, *sums = outs

    @pl.when(pl.program_id(0) == 0)
    def _():
        for g in sums:
            g[...] = jnp.zeros_like(g)

    rows = tile_rows()
    gated_rows, dz_rows = gated[rows, :], dz[rows, :]
    weight_sums(0, gated_rows, dz_rows, h, d, oc, sk, *sums)
    results(0, gated_rows, dz_rows, h, oc, now_w, res_w, skip_w, res, skip, part)


def last_kernel(base, place, h, d, oc, sk, z_now, dg, past_w, *rest):
    gated, dz, send0, send1, keep, g_taps, g_heads, g_bias = rest[3:]
    rows = tile_rows()
    gated_rows, dz_rows = gates(base, d, z_now, dg, past_w)
    gated[rows, :], dz[rows, :] = gated_rows, dz_rows
    weight_sums(base, gated_rows, dz_rows, h, d, oc, sk, g_taps, g_heads, g_bias)
    width = h.shape[1]

    @pl.when(pl.program_id(0) == pl.num_programs(0) - 1)
    def _():
        mine = place[0]
        for outs, side in (((send0, send1), 1 - mine), ((keep.at[0], keep.at[1]), mine)):
            for chip in range(16):
                x_lo, z = divmod(chip, 8)
                r = pl.multiple_of((2 * chip + side) * 8, 8)
                rr = pl.multiple_of((2 * chip + side) * 16, 16)
                pieces = (
                    g_taps[pl.ds(r, 8), :],
                    g_taps[pl.ds(width + r, 8), :],
                    g_heads[pl.ds(rr, 8), :width],
                    g_heads[pl.ds(rr + 8, 8), :width],
                    g_heads[pl.ds(rr, 8), width:],
                    g_heads[pl.ds(rr + 8, 8), width:],
                    g_bias[:, (chip // 2) * LANES : (chip // 2 + 1) * LANES],
                )
                at = 0
                for piece in pieces:
                    outs[z % 2][z // 2, x_lo, :, at : at + piece.shape[1]] = piece.astype(outs[0].dtype)
                    at += piece.shape[1]


def by_core_kernel(place, keep, came0, came1, keep_next, send_next):
    for odd, (near, far) in enumerate(((came0, came1), (came1, came0))):

        @pl.when(place[1] == odd)
        def _():
            keep_next[...] = keep[odd] + near[...].astype(F32)
            send_next[...] = (keep[1 - odd] + far[...].astype(F32)).astype(BF16)


def by_pair_kernel(place, keep, came, *outs):
    for k, out in enumerate(outs):
        at = lax.rem(place[2] + k, 4)
        out[...] = (keep[at] + came[at].astype(F32)).astype(out.dtype)


def total_of(own, one, two, three):
    return (own.astype(F32) + two.astype(F32)) + (one.astype(F32) + three.astype(F32))


def by_z_kernel(place, own, one, two, three, same, other):
    for out, at in ((same, place[3]), (other, 1 - place[3])):
        out[...] = total_of(own[at], one[at], two[at], three[at]).astype(out.dtype)


def by_x_kernel(own, one, two, three, out):
    out[...] = total_of(own[...], one[...], two[...], three[...]).astype(out.dtype)


def owner_kernel(place, own, one, two, three, g_now, g_past, g_res, g_skip, g_bias):
    width = g_res.shape[1]
    total = lambda at, n: total_of(*(a[:, at : at + n] for a in (own, one, two, three)))
    g_now[...] = total(0, 4 * width)
    g_past[...] = total(4 * width, 4 * width)
    for k in range(2):
        g_res[8 * k : 8 * k + 8, :] = total((8 + k) * width, width)
        g_skip[8 * k : 8 * k + 8, :] = total((10 + k) * width, width)
    sums = jnp.sum(total(12 * width, LANES), axis=0, keepdims=True)
    for m in range(4):

        @pl.when(place[4] == m)
        def _():
            g_bias[...] = sums[:, m * 32 : (m + 1) * 32]


def after_kernel(base, gated, dz, h, oc, now_w, past_w, res_w, skip_w, *rest):
    rows = tile_rows()
    dz_rows = dz[rows, :]
    *outs, back = rest[2:]
    results(base, gated[rows, :], dz_rows, h, oc, now_w, res_w, skip_w, *outs)
    back[...] = dot_t(dz_rows, past_w[...]).astype(BF16)


def finish_kernel(part, came, *refs):
    refs[-1][...] = (part[...] + came[...].astype(F32)).astype(BF16)


def call(body, name, steps, ins, in_specs, outs, out_specs, flops, aliases={}):
    return pl.pallas_call(
        body,
        out_shape=[kind(s, t) for s, t, *_ in outs for kind in [pltpu.HBM if _ else jax.ShapeDtypeStruct]],
        grid=(steps,),
        in_specs=in_specs,
        out_specs=out_specs,
        input_output_aliases=aliases,
        compiler_params=pltpu.CompilerParams(
            dimension_semantics=("arbitrary",), vmem_limit_bytes=24 << 20
        ),
        cost_estimate=pl.CostEstimate(flops=flops, bytes_accessed=flops >> 9, transcendentals=0),
        name=name,
    )(*ins)


def in_hbm(value):
    return pltpu.with_memory_space_constraint(value, pltpu.HBM)


def copy_rows_kernel(base, src, dst, sem):
    copy = pltpu.make_async_copy(src.at[pl.ds(base, dst.shape[0]), :], dst, sem)
    copy.start()
    copy.wait()


def copy_rows(value, base, rows):
    return pl.pallas_call(
        functools.partial(copy_rows_kernel, base),
        out_shape=jax.ShapeDtypeStruct((rows, value.shape[1]), value.dtype),
        in_specs=[pl.BlockSpec(memory_space=pl.ANY)],
        out_specs=VMEM,
        scratch_shapes=[pltpu.SemaphoreType.DMA],
        cost_estimate=pl.CostEstimate(flops=0, bytes_accessed=1 << 20, transcendentals=0),
        name="copy_rows",
    )(in_hbm(value))


def shift(value, steps):
    n = lax.axis_size("tm")
    return lax.ppermute(
        value, "tm", [(s, s + steps) for s in range(max(0, -steps), min(n, n - steps))]
    )


def exchange(value, axis, partner):
    return lax.ppermute(value, axis, [(i, partner(i)) for i in range(lax.axis_size(axis))])


def along_z(value, target):
    return exchange(value, "dp", lambda i: i // 16 * 16 + target(i // 2 % 8) * 2 + i % 2)


def along_y(value, k):
    return exchange(value, "tm", lambda i: (i + 2 * k) % 8)


def along_x(value, k):
    def target(i):
        x = (i // 32 % 2 * 2 + i % 32 // 16 + k) % 4
        return i // 64 * 64 + x // 2 * 32 + x % 2 * 16 + i % 16

    return lax.ppermute(value, ("tm", "dp"), [(i, target(i)) for i in range(256)])


def shards(history, now_w, past_w, gate_bias, res_w, skip_w, out_cot, skip_cot):
    _, total, width = history.shape
    h, oc, sk = history[0], out_cot[0], skip_cot[0]
    dp = lax.axis_index("dp")
    z = (dp // 2) % 8
    place = jnp.stack([dp % 2, z % 2, z // 2, dp // 16, dp % 4]).astype(jnp.int32)
    place, gate_bias = lax.optimization_barrier((place, gate_bias))
    first, last = CHUNKS
    macs = 2 * total * width * width

    d_first = shift(copy_rows(h, 0, first), 1)
    d_last = shift(copy_rows(h, first, last), 1)

    z_now, dg = call(
        before_kernel,
        "before",
        total // TILE,
        tuple(in_hbm(a) for a in (h, oc, sk, now_w, gate_bias[None, :], res_w, skip_w)),
        [pl.BlockSpec((TILE, width), lambda i: (i, 0))] * 3
        + [pl.BlockSpec(s, lambda i: (0, 0)) for s in (now_w.shape, (1, 4 * width), res_w.shape, skip_w.shape)],
        [((total, 4 * width), F32), ((total, 2 * width), F32)],
        [VMEM] * 2,
        macs * 8,
    )
    sums = [((2 * width, 4 * width), F32), ((2 * width, 2 * width), F32), ((8, 4 * width), F32)]
    rows_out = [
        ((total, width), BF16),
        ((total, width), BF16),
    ]
    tail_out = lambda n: [((n, width), F32, 1), ((n, width), BF16)]
    block = lambda base: pl.BlockSpec((TILE, width), lambda i: (base // TILE + i, 0))
    back0, gated0, dz0 = call(
        first_kernel,
        "first",
        first // TILE,
        (d_first, z_now, dg, past_w),
        [VMEM] * 4,
        [((first, width), BF16), ((first, 2 * width), BF16), ((first, 4 * width), BF16)],
        [block(0)] + [VMEM] * 2,
        macs * 12 * first // total,
    )
    res, skip, part0, g_taps, g_heads, g_bias = call(
        rest_kernel,
        "rest",
        first // TILE,
        (gated0, dz0, h, d_first, oc, sk, now_w, res_w, skip_w),
        [VMEM] * 9,
        rows_out + tail_out(first)[:1] + sums,
        [block(0)] * 3 + [VMEM] * 3,
        1 << 20,
    )
    block_shape = (8, 12 * width + LANES)
    packed = (2, 4, 2, *block_shape)
    came0 = shift(back0, -1)
    gated, dz, send0, send1, keep, *_ = call(
        functools.partial(last_kernel, first),
        "last",
        last // TILE,
        (place, h, d_last, oc, sk, z_now, dg, past_w, g_taps, g_heads, g_bias),
        [pl.BlockSpec(memory_space=pltpu.SMEM)] + [VMEM] * 10,
        [((last, 2 * width), BF16), ((last, 4 * width), BF16), (packed[1:], BF16), (packed[1:], BF16), (packed, F32)]
        + sums,
        [VMEM] * 8,
        1 << 20,
        {8: 5, 9: 6, 10: 7},
    )
    halves = [exchange(v, "dp", lambda i: i ^ 1) for v in (send0, send1)]
    *halves, came0 = lax.optimization_barrier((*halves, came0))
    smem = pl.BlockSpec(memory_space=pltpu.SMEM)
    step = lambda body, name, ins, outs, flops=1 << 20: call(
        body, name, 1, ins, [smem] * (ins[0] is place) + [VMEM] * (len(ins) - (ins[0] is place)), outs,
        [VMEM] * len(outs), flops,
    )
    keep, send = step(by_core_kernel, "by_core", (place, keep, *halves), [(packed[1:], F32), (packed[1:], BF16)])
    came = along_z(send, lambda z: z ^ 1)
    gated, dz, _ = lax.optimization_barrier((gated, dz, send))
    res, skip, part1, back1 = call(
        functools.partial(after_kernel, first),
        "after",
        last // TILE,
        (gated, dz, h, oc, now_w, past_w, res_w, skip_w, res, skip),
        [VMEM] * 8 + [pl.BlockSpec(memory_space=pl.ANY)] * 2,
        rows_out + tail_out(last),
        [block(first)] * 2 + [block(0)] * 2,
        macs * 12 * last // total,
        {8: 0, 9: 1},
    )

    own, *others = step(
        by_pair_kernel, "by_pair", (place, keep, came), [(packed[2:], F32)] + [(packed[2:], BF16)] * 3,
        macs * 1000,
    )
    one, two, three = (along_z(v, lambda z, k=k: (z + 2 * k) % 8) for k, v in enumerate(others, 1))
    finish = lambda base, rows, ins, aliases: call(
        finish_kernel, "finish", rows // TILE, ins,
        [block(0)] * 2 + [pl.BlockSpec(memory_space=pl.ANY)] * len(aliases),
        [((total, width), BF16)], [block(base)], macs, aliases,
    )[0]
    grad_in = finish(0, first, (part0, came0), {})
    own, one, two, three, grad_in = lax.optimization_barrier((own, one, two, three, grad_in))
    grad_in = finish(first, last, (part1, shift(back1, -1), grad_in), {2: 0})
    same, other = step(
        by_z_kernel, "by_z", (place, own, one, two, three), [(block_shape, BF16)] * 2
    )
    (mine,) = step(
        by_x_kernel, "by_x", (same, along_x(other, 1), along_x(same, 2), along_x(other, 3)), [(block_shape, BF16)]
    )
    others = [along_y(mine, k) for k in (1, 2, 3)]
    *others, grad_in = lax.optimization_barrier((*others, grad_in))
    g_now, g_past, g_res, g_skip, g_bias = step(
        owner_kernel,
        "owner",
        (place, mine, *others),
        [((8, 4 * width), F32)] * 2 + [((16, width), F32)] * 2 + [((1, 32), F32)],
    )
    return res[None], skip[None], grad_in[None], g_now, g_past, g_bias[0], g_res, g_skip


def solution(mesh):
    rows, whole = P("dp", "tm", None), P()
    return jax.shard_map(
        shards,
        mesh=mesh,
        in_specs=(rows, whole, whole, whole, whole, whole, rows, rows),
        out_specs=(rows, rows, rows, P("dp", None), P("dp", None), P("dp"), P("dp", None), P("dp", None)),
        check_vma=False,
    )
```

```python
import functools

import jax
import jax.numpy as jnp
from jax import lax
from jax.experimental import pallas as pl
from jax.experimental.pallas import tpu as pltpu
from jax.sharding import PartitionSpec as P

BF16, F32 = jnp.bfloat16, jnp.float32
TILE = 512
LANES = 128
VMEM = pl.BlockSpec(memory_space=pltpu.VMEM)


def dot(a, b):
    return jnp.dot(a, b, preferred_element_type=F32)


def dot_t(a, b):
    return lax.dot_general(a, b, (((1,), (1,)), ((), ())), preferred_element_type=F32)


def dot_rows(a, b):
    return lax.dot_general(a, b, (((0,), (0,)), ((), ())), preferred_element_type=F32)


def tile_rows(base=0):
    return pl.ds(pl.multiple_of(base + pl.program_id(0) * TILE, TILE), TILE)


def before_kernel(h, oc, sk, now_w, bias, res_w, skip_w, z_now, dg):
    rows = tile_rows()
    z_now[rows, :] = dot(h[...], now_w[...]) + bias[...]
    dg[rows, :] = dot_t(oc[...], res_w[...]) + dot_t(sk[...], skip_w[...])


def gates(rows, d, z_now, dg, past_w):
    z = z_now[rows, :] + dot(d[rows, :], past_w[...])
    half = z.shape[1] // 2
    th = jnp.tanh(z[:, :half])
    sg = 0.5 * jnp.tanh(0.5 * z[:, half:]) + 0.5
    ts = th * sg
    dgated = dg[rows, :]
    dza = dgated * (sg - ts * th)
    dzb = dgated * (ts - ts * sg)
    return ts.astype(BF16), jnp.concatenate([dza.astype(BF16), dzb.astype(BF16)], axis=1)


def weight_sums(rows, gated, dz, h, d, oc, sk):
    return (
        dot_rows(jnp.concatenate([h[rows, :], d[rows, :]], axis=1), dz),
        dot_rows(gated, jnp.concatenate([oc[rows, :], sk[rows, :]], axis=1)),
        jnp.sum(dz.astype(F32).reshape(-1, 8, dz.shape[1]), axis=0),
    )


def results(base, gated, dz, h, oc, now_w, res_w, skip_w, res, skip, part):
    rows = tile_rows(base)
    res[...] = (h[rows, :].astype(F32) + dot(gated, res_w[...])).astype(BF16)
    skip[...] = dot(gated, skip_w[...]).astype(BF16)
    part[...] = oc[rows, :].astype(F32) + dot_t(dz, now_w[...])


def last_kernel(place, h, d, oc, sk, z_now, dg, past_w, *rest):
    gated, dz, send0, send1, keep, *sums = rest
    g_taps, g_heads, g_bias = sums
    width = h.shape[1]
    before = None
    for tile in range(h.shape[0] // TILE + 1):
        now = None
        if tile * TILE < h.shape[0]:
            rows = slice(tile * TILE, (tile + 1) * TILE)
            now = (rows, *gates(rows, d, z_now, dg, past_w))
            gated[rows, :], dz[rows, :] = now[1:]
        if before is not None:
            for g, term in zip(sums, weight_sums(*before, h, d, oc, sk)):
                g[...] = term if tile == 1 else g[...] + term
        before = now

    @pl.when(pl.program_id(0) == pl.num_programs(0) - 1)
    def _():
        mine = place[0]
        for outs, side in (((send0, send1), 1 - mine), ((keep.at[0], keep.at[1]), mine)):
            for chip in range(16):
                x_lo, z = divmod(chip, 8)
                r = pl.multiple_of((2 * chip + side) * 8, 8)
                rr = pl.multiple_of((2 * chip + side) * 16, 16)
                pieces = (
                    g_taps[pl.ds(r, 8), :],
                    g_taps[pl.ds(width + r, 8), :],
                    g_heads[pl.ds(rr, 8), :width],
                    g_heads[pl.ds(rr + 8, 8), :width],
                    g_heads[pl.ds(rr, 8), width:],
                    g_heads[pl.ds(rr + 8, 8), width:],
                    g_bias[:, (chip // 2) * LANES : (chip // 2 + 1) * LANES],
                )
                at = 0
                for piece in pieces:
                    outs[z % 2][z // 2, x_lo, :, at : at + piece.shape[1]] = piece.astype(outs[0].dtype)
                    at += piece.shape[1]


def by_core_kernel(place, keep, came0, came1, keep_next, send_next):
    for odd, (near, far) in enumerate(((came0, came1), (came1, came0))):

        @pl.when(place[1] == odd)
        def _():
            keep_next[...] = keep[odd] + near[...].astype(F32)
            send_next[...] = (keep[1 - odd] + far[...].astype(F32)).astype(BF16)


def by_pair_kernel(place, keep, came, *outs):
    for k, out in enumerate(outs):
        at = lax.rem(place[2] + k, 4)
        out[...] = (keep[at] + came[at].astype(F32)).astype(out.dtype)


def total_of(own, one, two, three):
    return (own.astype(F32) + two.astype(F32)) + (one.astype(F32) + three.astype(F32))


def by_z_kernel(place, own, one, two, three, same, other):
    for out, at in ((same, place[3]), (other, 1 - place[3])):
        out[...] = total_of(own[at], one[at], two[at], three[at]).astype(out.dtype)


def by_x_kernel(own, one, two, three, out):
    out[...] = total_of(own[...], one[...], two[...], three[...]).astype(out.dtype)


def owner_kernel(place, own, one, two, three, g_now, g_past, g_res, g_skip, g_bias):
    width = g_res.shape[1]
    total = lambda at, n: total_of(*(a[:, at : at + n] for a in (own, one, two, three)))
    g_now[...] = total(0, 4 * width)
    g_past[...] = total(4 * width, 4 * width)
    for k in range(2):
        g_res[8 * k : 8 * k + 8, :] = total((8 + k) * width, width)
        g_skip[8 * k : 8 * k + 8, :] = total((10 + k) * width, width)
    sums = jnp.sum(total(12 * width, LANES), axis=0, keepdims=True)
    for m in range(4):

        @pl.when(place[4] == m)
        def _():
            g_bias[...] = sums[:, m * 32 : (m + 1) * 32]


def back_kernel(dz, past_w, back):
    back[...] = dot_t(dz[tile_rows(), :], past_w[...]).astype(BF16)


def results_kernel(gated, dz, h, oc, now_w, res_w, skip_w, *outs):
    rows = tile_rows()
    results(0, gated[rows, :], dz[rows, :], h, oc, now_w, res_w, skip_w, *outs)


def finish_kernel(part, came, *refs):
    refs[-1][...] = (part[...] + came[...].astype(F32)).astype(BF16)


def call(body, name, steps, ins, in_specs, outs, out_specs, flops, aliases={}):
    return pl.pallas_call(
        body,
        out_shape=[kind(s, t) for s, t, *_ in outs for kind in [pltpu.HBM if _ else jax.ShapeDtypeStruct]],
        grid=(steps,),
        in_specs=in_specs,
        out_specs=out_specs,
        input_output_aliases=aliases,
        compiler_params=pltpu.CompilerParams(
            dimension_semantics=("arbitrary",), vmem_limit_bytes=24 << 20
        ),
        cost_estimate=pl.CostEstimate(flops=flops, bytes_accessed=flops >> 9, transcendentals=0),
        name=name,
    )(*ins)


def in_hbm(value):
    return pltpu.with_memory_space_constraint(value, pltpu.HBM)


def shift(value, steps):
    n = lax.axis_size("tm")
    return lax.ppermute(
        value, "tm", [(s, s + steps) for s in range(max(0, -steps), min(n, n - steps))]
    )


def exchange(value, axis, partner):
    return lax.ppermute(value, axis, [(i, partner(i)) for i in range(lax.axis_size(axis))])


def along_z(value, target):
    return exchange(value, "dp", lambda i: i // 16 * 16 + target(i // 2 % 8) * 2 + i % 2)


def along_y(value, k):
    return exchange(value, "tm", lambda i: (i + 2 * k) % 8)


def along_x(value, k):
    def target(i):
        x = (i // 32 % 2 * 2 + i % 32 // 16 + k) % 4
        return i // 64 * 64 + x // 2 * 32 + x % 2 * 16 + i % 16

    return lax.ppermute(value, ("tm", "dp"), [(i, target(i)) for i in range(256)])


def shards(history, now_w, past_w, gate_bias, res_w, skip_w, out_cot, skip_cot):
    _, total, width = history.shape
    h, oc, sk = history[0], out_cot[0], skip_cot[0]
    dp = lax.axis_index("dp")
    z = (dp // 2) % 8
    place = jnp.stack([dp % 2, z % 2, z // 2, dp // 16, dp % 4]).astype(jnp.int32)
    place, gate_bias = lax.optimization_barrier((place, gate_bias))
    macs = 2 * total * width * width
    d = shift(history, 1)[0]
    z_now, dg = call(
        before_kernel,
        "before",
        total // TILE,
        tuple(in_hbm(a) for a in (h, oc, sk, now_w, gate_bias[None, :], res_w, skip_w)),
        [pl.BlockSpec((TILE, width), lambda i: (i, 0))] * 3
        + [pl.BlockSpec(s, lambda i: (0, 0)) for s in (now_w.shape, (1, 4 * width), res_w.shape, skip_w.shape)],
        [((total, 4 * width), F32), ((total, 2 * width), F32)],
        [VMEM] * 2,
        macs * 8,
    )
    sums = [((2 * width, 4 * width), F32), ((2 * width, 2 * width), F32), ((8, 4 * width), F32)]
    rows_out = [
        ((total, width), BF16),
        ((total, width), BF16),
    ]
    block = lambda base: pl.BlockSpec((TILE, width), lambda i: (base // TILE + i, 0))
    block_shape = (8, 12 * width + LANES)
    packed = (2, 4, 2, *block_shape)
    gated, dz, send0, send1, keep, *_ = call(
        last_kernel,
        "sums",
        1,
        (place, h, d, oc, sk, z_now, dg, past_w),
        [pl.BlockSpec(memory_space=pltpu.SMEM)] + [VMEM] * 7,
        [((total, 2 * width), BF16), ((total, 4 * width), BF16)]
        + [(packed[1:], BF16), (packed[1:], BF16), (packed, F32)]
        + sums,
        [VMEM] * 8,
        macs * 16,
    )
    halves = [exchange(v, "dp", lambda i: i ^ 1) for v in (send0, send1)]
    smem = pl.BlockSpec(memory_space=pltpu.SMEM)
    step = lambda body, name, ins, outs, flops=1 << 20: call(
        body, name, 1, ins, [smem] * (ins[0] is place) + [VMEM] * (len(ins) - (ins[0] is place)), outs,
        [VMEM] * len(outs), flops,
    )
    keep, send = step(by_core_kernel, "by_core", (place, keep, *halves), [(packed[1:], F32), (packed[1:], BF16)])
    came = along_z(send, lambda z: z ^ 1)
    gated, dz, _ = lax.optimization_barrier((gated, dz, send))
    (back,) = call(
        back_kernel, "back", total // TILE, (dz, past_w), [VMEM] * 2, [((total, width), BF16)],
        [block(0)], 1 << 20,
    )
    own, *others = step(
        by_pair_kernel, "by_pair", (place, keep, came), [(packed[2:], F32)] + [(packed[2:], BF16)] * 3,
        macs * 1000,
    )
    one, two, three = (along_z(v, lambda z, k=k: (z + 2 * k) % 8) for k, v in enumerate(others, 1))
    gated, dz, *_ = lax.optimization_barrier((gated, dz, back, *others))
    res, skip, part = call(
        results_kernel,
        "results",
        total // TILE,
        (gated, dz, h, oc, now_w, res_w, skip_w),
        [VMEM] * 7,
        rows_out + [((total, width), F32, 1)],
        [block(0)] * 3,
        1 << 20,
    )
    one, two, three, part = lax.optimization_barrier((one, two, three, part))
    moved = shift(back, -1)
    half = total // 2
    finish = lambda base, ins, aliases: call(
        finish_kernel, "finish", half // TILE, ins,
        [block(base)] * 2 + [pl.BlockSpec(memory_space=pl.ANY)] * len(aliases),
        [((total, width), BF16)], [block(base)], macs, aliases,
    )[0]
    first_half = finish(0, (part, moved), {})
    same, other = step(
        by_z_kernel, "by_z", (place, own, one, two, three), [(block_shape, BF16)] * 2
    )
    xs = along_x(other, 1), along_x(same, 2), along_x(other, 3)
    *xs, first_half = lax.optimization_barrier((*xs, first_half))
    (mine,) = step(by_x_kernel, "by_x", (same, *xs), [(block_shape, BF16)])
    grad_in_whole = finish(half, (part, moved, first_half), {2: 0})
    others = [along_y(mine, k) for k in (1, 2, 3)]
    *others, grad_in = lax.optimization_barrier((*others, grad_in_whole))
    g_now, g_past, g_res, g_skip, g_bias = step(
        owner_kernel,
        "owner",
        (place, mine, *others),
        [((8, 4 * width), F32)] * 2 + [((16, width), F32)] * 2 + [((1, 32), F32)],
    )
    return res[None], skip[None], grad_in[None], g_now, g_past, g_bias[0], g_res, g_skip


def solution(mesh):
    rows, whole = P("dp", "tm", None), P()
    return jax.shard_map(
        shards,
        mesh=mesh,
        in_specs=(rows, whole, whole, whole, whole, whole, rows, rows),
        out_specs=(rows, rows, rows, P("dp", None), P("dp", None), P("dp"), P("dp", None), P("dp", None)),
        check_vma=False,
    )
```

```python
import functools

import jax
import jax.numpy as jnp
from jax import lax
from jax.experimental import pallas as pl
from jax.experimental.pallas import tpu as pltpu
from jax.sharding import PartitionSpec as P

BF16, F32 = jnp.bfloat16, jnp.float32
TILE = 512
CHUNKS = (1024, 1024)
LANES = 128
VMEM = pl.BlockSpec(memory_space=pltpu.VMEM)


def dot(a, b):
    return jnp.dot(a, b, preferred_element_type=F32)


def dot_t(a, b):
    return lax.dot_general(a, b, (((1,), (1,)), ((), ())), preferred_element_type=F32)


def dot_rows(a, b):
    return lax.dot_general(a, b, (((0,), (0,)), ((), ())), preferred_element_type=F32)


def tile_rows(base=0):
    return pl.ds(pl.multiple_of(base + pl.program_id(0) * TILE, TILE), TILE)


def before_kernel(h, oc, sk, now_w, bias, res_w, skip_w, z_now, dg):
    rows = tile_rows()
    z_now[rows, :] = dot(h[...], now_w[...]) + bias[...]
    dg[rows, :] = dot_t(oc[...], res_w[...]) + dot_t(sk[...], skip_w[...])


def gates(base, h, d, oc, sk, z_now, dg, past_w, g_taps, g_heads, g_bias):
    rows = tile_rows(base)
    delayed = d[tile_rows(), :]
    z = z_now[rows, :] + dot(delayed, past_w[...])
    half = z.shape[1] // 2
    th = jnp.tanh(z[:, :half])
    sg = 0.5 * jnp.tanh(0.5 * z[:, half:]) + 0.5
    ts = th * sg
    gated = ts.astype(BF16)
    dgated = dg[rows, :]
    dza = dgated * (sg - ts * th)
    dzb = dgated * (ts - ts * sg)
    dz = jnp.concatenate([dza.astype(BF16), dzb.astype(BF16)], axis=1)
    g_taps[...] += dot_rows(jnp.concatenate([h[rows, :], delayed], axis=1), dz)
    g_heads[...] += dot_rows(gated, jnp.concatenate([oc[rows, :], sk[rows, :]], axis=1))
    g_bias[...] += jnp.sum(dz.astype(F32).reshape(-1, 8, 2 * half), axis=0)
    return gated, dz


def results(base, gated, dz, h, oc, now_w, past_w, res_w, skip_w, res, skip, part, back):
    rows = tile_rows(base)
    res[...] = (h[rows, :].astype(F32) + dot(gated, res_w[...])).astype(BF16)
    skip[...] = dot(gated, skip_w[...]).astype(BF16)
    part[...] = oc[rows, :].astype(F32) + dot_t(dz, now_w[...])
    back[...] = dot_t(dz, past_w[...]).astype(BF16)


def first_kernel(h, d, oc, sk, z_now, dg, now_w, past_w, res_w, skip_w, *outs):
    res, skip, part, back, g_taps, g_heads, g_bias = outs

    @pl.when(pl.program_id(0) == 0)
    def _():
        for g in (g_taps, g_heads, g_bias):
            g[...] = jnp.zeros_like(g)

    gated, dz = gates(0, h, d, oc, sk, z_now, dg, past_w, g_taps, g_heads, g_bias)
    results(0, gated, dz, h, oc, now_w, past_w, res_w, skip_w, res, skip, part, back)


def last_kernel(base, place, h, d, oc, sk, z_now, dg, past_w, *rest):
    gated, dz, send0, send1, keep, g_taps, g_heads, g_bias = rest[3:]
    rows = tile_rows()
    gated[rows, :], dz[rows, :] = gates(
        base, h, d, oc, sk, z_now, dg, past_w, g_taps, g_heads, g_bias
    )
    width = h.shape[1]

    @pl.when(pl.program_id(0) == pl.num_programs(0) - 1)
    def _():
        mine = place[0]
        for outs, side in (((send0, send1), 1 - mine), ((keep.at[0], keep.at[1]), mine)):
            for chip in range(16):
                x_lo, z = divmod(chip, 8)
                r = pl.multiple_of((2 * chip + side) * 8, 8)
                rr = pl.multiple_of((2 * chip + side) * 16, 16)
                pieces = (
                    g_taps[pl.ds(r, 8), :],
                    g_taps[pl.ds(width + r, 8), :],
                    g_heads[pl.ds(rr, 8), :width],
                    g_heads[pl.ds(rr + 8, 8), :width],
                    g_heads[pl.ds(rr, 8), width:],
                    g_heads[pl.ds(rr + 8, 8), width:],
                    g_bias[:, (chip // 2) * LANES : (chip // 2 + 1) * LANES],
                )
                at = 0
                for piece in pieces:
                    outs[z % 2][z // 2, x_lo, :, at : at + piece.shape[1]] = piece.astype(outs[0].dtype)
                    at += piece.shape[1]


def by_core_kernel(place, keep, came0, came1, keep_next, send_next):
    for odd, (near, far) in enumerate(((came0, came1), (came1, came0))):

        @pl.when(place[1] == odd)
        def _():
            keep_next[...] = keep[odd] + near[...].astype(F32)
            send_next[...] = (keep[1 - odd] + far[...].astype(F32)).astype(BF16)


def by_pair_kernel(place, keep, came, *outs):
    for k, out in enumerate(outs):
        at = lax.rem(place[2] + k, 4)
        out[...] = (keep[at] + came[at].astype(F32)).astype(out.dtype)


def total_of(own, one, two, three):
    return (own.astype(F32) + two.astype(F32)) + (one.astype(F32) + three.astype(F32))


def by_z_kernel(place, own, one, two, three, same, other):
    for out, at in ((same, place[3]), (other, 1 - place[3])):
        out[...] = total_of(own[at], one[at], two[at], three[at]).astype(out.dtype)


def by_x_kernel(own, one, two, three, out):
    out[...] = total_of(own[...], one[...], two[...], three[...]).astype(out.dtype)


def owner_kernel(place, own, one, two, three, g_now, g_past, g_res, g_skip, g_bias):
    width = g_res.shape[1]
    total = lambda at, n: total_of(*(a[:, at : at + n] for a in (own, one, two, three)))
    g_now[...] = total(0, 4 * width)
    g_past[...] = total(4 * width, 4 * width)
    for k in range(2):
        g_res[8 * k : 8 * k + 8, :] = total((8 + k) * width, width)
        g_skip[8 * k : 8 * k + 8, :] = total((10 + k) * width, width)
    sums = jnp.sum(total(12 * width, LANES), axis=0, keepdims=True)
    for m in range(4):

        @pl.when(place[4] == m)
        def _():
            g_bias[...] = sums[:, m * 32 : (m + 1) * 32]


def after_kernel(base, gated, dz, h, oc, now_w, past_w, res_w, skip_w, *rest):
    rows = tile_rows()
    results(base, gated[rows, :], dz[rows, :], h, oc, now_w, past_w, res_w, skip_w, *rest[2:])


def finish_kernel(part, came, *refs):
    refs[-1][...] = (part[...] + came[...].astype(F32)).astype(BF16)


def call(body, name, steps, ins, in_specs, outs, out_specs, flops, aliases={}):
    return pl.pallas_call(
        body,
        out_shape=[kind(s, t) for s, t, *_ in outs for kind in [pltpu.HBM if _ else jax.ShapeDtypeStruct]],
        grid=(steps,),
        in_specs=in_specs,
        out_specs=out_specs,
        input_output_aliases=aliases,
        compiler_params=pltpu.CompilerParams(
            dimension_semantics=("arbitrary",), vmem_limit_bytes=24 << 20
        ),
        cost_estimate=pl.CostEstimate(flops=flops, bytes_accessed=flops >> 9, transcendentals=0),
        name=name,
    )(*ins)


def in_hbm(value):
    return pltpu.with_memory_space_constraint(value, pltpu.HBM)


def copy_rows_kernel(base, src, dst, sem):
    copy = pltpu.make_async_copy(src.at[pl.ds(base, dst.shape[0]), :], dst, sem)
    copy.start()
    copy.wait()


def copy_rows(value, base, rows):
    return pl.pallas_call(
        functools.partial(copy_rows_kernel, base),
        out_shape=jax.ShapeDtypeStruct((rows, value.shape[1]), value.dtype),
        in_specs=[pl.BlockSpec(memory_space=pl.ANY)],
        out_specs=VMEM,
        scratch_shapes=[pltpu.SemaphoreType.DMA],
        cost_estimate=pl.CostEstimate(flops=0, bytes_accessed=1 << 20, transcendentals=0),
        name="copy_rows",
    )(in_hbm(value))


def shift(value, steps):
    n = lax.axis_size("tm")
    return lax.ppermute(
        value, "tm", [(s, s + steps) for s in range(max(0, -steps), min(n, n - steps))]
    )


def exchange(value, axis, partner):
    return lax.ppermute(value, axis, [(i, partner(i)) for i in range(lax.axis_size(axis))])


def along_z(value, target):
    return exchange(value, "dp", lambda i: i // 16 * 16 + target(i // 2 % 8) * 2 + i % 2)


def along_y(value, k):
    return exchange(value, "tm", lambda i: (i + 2 * k) % 8)


def along_x(value, k):
    def target(i):
        x = (i // 32 % 2 * 2 + i % 32 // 16 + k) % 4
        return i // 64 * 64 + x // 2 * 32 + x % 2 * 16 + i % 16

    return lax.ppermute(value, ("tm", "dp"), [(i, target(i)) for i in range(256)])


def shards(history, now_w, past_w, gate_bias, res_w, skip_w, out_cot, skip_cot):
    _, total, width = history.shape
    h, oc, sk = history[0], out_cot[0], skip_cot[0]
    dp = lax.axis_index("dp")
    z = (dp // 2) % 8
    place = jnp.stack([dp % 2, z % 2, z // 2, dp // 16, dp % 4]).astype(jnp.int32)
    place, gate_bias = lax.optimization_barrier((place, gate_bias))
    first, last = CHUNKS
    macs = 2 * total * width * width

    d_first = shift(copy_rows(h, 0, first), 1)
    d_last = shift(copy_rows(h, first, last), 1)

    z_now, dg = call(
        before_kernel,
        "before",
        total // TILE,
        tuple(in_hbm(a) for a in (h, oc, sk, now_w, gate_bias[None, :], res_w, skip_w)),
        [pl.BlockSpec((TILE, width), lambda i: (i, 0))] * 3
        + [pl.BlockSpec(s, lambda i: (0, 0)) for s in (now_w.shape, (1, 4 * width), res_w.shape, skip_w.shape)],
        [((total, 4 * width), F32), ((total, 2 * width), F32)],
        [VMEM] * 2,
        macs * 8,
    )
    sums = [((2 * width, 4 * width), F32), ((2 * width, 2 * width), F32), ((8, 4 * width), F32)]
    rows_out = [
        ((total, width), BF16),
        ((total, width), BF16),
    ]
    tail_out = lambda n: [((n, width), F32, 1), ((n, width), BF16)]
    block = lambda base: pl.BlockSpec((TILE, width), lambda i: (base // TILE + i, 0))
    res, skip, part0, back0, g_taps, g_heads, g_bias = call(
        first_kernel,
        "first",
        first // TILE,
        (h, d_first, oc, sk, z_now, dg, now_w, past_w, res_w, skip_w),
        [VMEM] * 10,
        rows_out + tail_out(first) + sums,
        [block(0)] * 4 + [VMEM] * 3,
        macs * 28 * first // total,
    )
    block_shape = (8, 12 * width + LANES)
    packed = (2, 4, 2, *block_shape)
    came0 = shift(back0, -1)
    gated, dz, send0, send1, keep, *_ = call(
        functools.partial(last_kernel, first),
        "last",
        last // TILE,
        (place, h, d_last, oc, sk, z_now, dg, past_w, g_taps, g_heads, g_bias),
        [pl.BlockSpec(memory_space=pltpu.SMEM)] + [VMEM] * 10,
        [((last, 2 * width), BF16), ((last, 4 * width), BF16), (packed[1:], BF16), (packed[1:], BF16), (packed, F32)]
        + sums,
        [VMEM] * 8,
        1 << 20,
        {8: 5, 9: 6, 10: 7},
    )
    halves = [exchange(v, "dp", lambda i: i ^ 1) for v in (send0, send1)]
    *halves, came0 = lax.optimization_barrier((*halves, came0))
    smem = pl.BlockSpec(memory_space=pltpu.SMEM)
    step = lambda body, name, ins, outs, flops=1 << 20: call(
        body, name, 1, ins, [smem] * (ins[0] is place) + [VMEM] * (len(ins) - (ins[0] is place)), outs,
        [VMEM] * len(outs), flops,
    )
    keep, send = step(by_core_kernel, "by_core", (place, keep, *halves), [(packed[1:], F32), (packed[1:], BF16)])
    came = along_z(send, lambda z: z ^ 1)
    gated, dz, _ = lax.optimization_barrier((gated, dz, send))
    res, skip, part1, back1 = call(
        functools.partial(after_kernel, first),
        "after",
        last // TILE,
        (gated, dz, h, oc, now_w, past_w, res_w, skip_w, res, skip),
        [VMEM] * 8 + [pl.BlockSpec(memory_space=pl.ANY)] * 2,
        rows_out + tail_out(last),
        [block(first)] * 2 + [block(0)] * 2,
        macs * 12 * last // total,
        {8: 0, 9: 1},
    )

    own, *others = step(
        by_pair_kernel, "by_pair", (place, keep, came), [(packed[2:], F32)] + [(packed[2:], BF16)] * 3,
        macs * 1000,
    )
    one, two, three = (along_z(v, lambda z, k=k: (z + 2 * k) % 8) for k, v in enumerate(others, 1))
    finish = lambda base, rows, ins, aliases: call(
        finish_kernel, "finish", rows // TILE, ins,
        [block(0)] * 2 + [pl.BlockSpec(memory_space=pl.ANY)] * len(aliases),
        [((total, width), BF16)], [block(base)], macs, aliases,
    )[0]
    grad_in = finish(0, first, (part0, came0), {})
    own, one, two, three, grad_in = lax.optimization_barrier((own, one, two, three, grad_in))
    grad_in = finish(first, last, (part1, shift(back1, -1), grad_in), {2: 0})
    same, other = step(
        by_z_kernel, "by_z", (place, own, one, two, three), [(block_shape, BF16)] * 2
    )
    xs = along_x(other, 1), along_x(same, 2), along_x(other, 3)
    *xs, grad_in = lax.optimization_barrier((*xs, grad_in))
    (mine,) = step(by_x_kernel, "by_x", (same, *xs), [(block_shape, BF16)])
    others = [along_y(mine, k) for k in (1, 2, 3)]
    g_now, g_past, g_res, g_skip, g_bias = step(
        owner_kernel,
        "owner",
        (place, mine, *others),
        [((8, 4 * width), F32)] * 2 + [((16, width), F32)] * 2 + [((1, 32), F32)],
    )
    return res[None], skip[None], grad_in[None], g_now, g_past, g_bias[0], g_res, g_skip


def solution(mesh):
    rows, whole = P("dp", "tm", None), P()
    return jax.shard_map(
        shards,
        mesh=mesh,
        in_specs=(rows, whole, whole, whole, whole, whole, rows, rows),
        out_specs=(rows, rows, rows, P("dp", None), P("dp", None), P("dp"), P("dp", None), P("dp", None)),
        check_vma=False,
    )
```
